32 devices in a mesh: row: 8 (over z, y), col: 4 (over x, core).
Axes of the slice: x: 2, y: 2, z: 4, core: 2. Of those that a mesh axis runs over, the one named last changes fastest.
Arguments:
- amps: bfloat16 [1024, 4096], P('col', 'row'), may hold values from -6 to 6, as said below
- ints: bfloat16 [2048, 8192], P('col', 'row'), may hold values from -0.125 to 0.125
- block_list: int32 [4, 4], replicated, may hold values from 0 to 1, as said below
Outputs:
- residual: float32 [32, 256, 1024], P(('row', 'col'))
The draws below stay inside these ranges and needn't reach their ends.
Inputs may be any that keep to these rules, and one draw needn't show every extreme that they name: amps blocks (c, r) and (c, r2) are equal whenever r and r2 agree mod 4. block_list[c, k] is 1 exactly when occupied block c and cd block k carry the same irrep; each block carries one of min(8, 2) irreps, every irrep equally often among occupied blocks and among cd blocks.
All inputs are finite; a program needn't handle non-finite values.
Results may differ from the reference program's by a relative error of at most 0.0003.
Values may be sent and summed in bfloat16 or wider, within the bound.
No kernel may reach another device: no remote copies, remote signals or barrier semaphores. Data moves between devices by JAX's collectives and lax.ppermute only.
A program may use at most 64 MiB of HBM per device.

```python
import jax
import jax.numpy as jnp

KB = 512
OCC_DEV = 256
AB_DEV = 1024
STEPS = 4
AB = 8192
INT_ROWS = 2048
N_ROW = 8
N_COL = 4


def draw_amps(key, part):
    base = jnp.clip(jax.random.normal(key, (N_COL, OCC_DEV, N_COL, KB), jnp.float32), -6.0, 6.0)
    col_ids = jnp.arange(N_COL, dtype=jnp.int32)
    row_ids = jnp.arange(N_ROW, dtype=jnp.int32)
    block_ids = (row_ids[None, :] + col_ids[:, None]) % N_COL
    placed = base[col_ids[:, None], :, block_ids]
    return placed.transpose(0, 2, 1, 3).reshape(N_COL * OCC_DEV, N_ROW * KB).astype(jnp.bfloat16)


def draw_block_list(key, part):
    kinds = min(8, N_COL // 2)
    occupied = jax.random.permutation(jax.random.fold_in(key, 11), N_COL) % kinds
    virtual = jax.random.permutation(jax.random.fold_in(key, 23), N_COL) % kinds
    return (occupied[:, None] == virtual[None, :]).astype(jnp.int32)


def steps_of(key, extent, shards, least, top_value):
    def one(position, blocks):
        heights = jax.random.uniform(jax.random.fold_in(jax.random.fold_in(key, 6), position), (blocks,), jnp.float32, least / len(shards), top_value / len(shards))
        return jnp.repeat(jnp.exp(heights), extent[position] // blocks).reshape((-1,) + (1,) * (len(extent) - position - 1))

    factor_of = one(*shards[0])
    for cut in shards[1:]:
        factor_of = factor_of * one(*cut)
    return factor_of


def bell_draw(key, dims, spread, limit, pieces=(), held_as=jnp.bfloat16):
    factor_of = steps_of(key, dims, pieces, -0.22, 0.18) if pieces else 1.0
    values = jax.random.normal(key, dims, jnp.float32) * spread * factor_of
    return jnp.minimum(jnp.maximum(values, -limit), limit).astype(held_as)


def setup_inputs(seed: int = 0) -> dict:
    key_of = jax.random.split(jax.random.key(seed), 4)
    return {
        "amps": draw_amps(jax.random.fold_in(key_of[3], 71), 0),
        "ints": bell_draw(key_of[1], (INT_ROWS, AB), (KB * 4) ** -0.5, 0.125, ((0, 4), (1, 8))),
        "block_list": draw_block_list(jax.random.fold_in(key_of[3], 71), 0),
    }


def reference(amps, ints, block_list):
    amp_grid = amps.astype(jnp.float32).reshape(N_COL, OCC_DEV, N_ROW, KB).transpose(0, 2, 1, 3)
    int_grid = ints.astype(jnp.float32).reshape(N_COL, KB, N_ROW, AB_DEV).transpose(0, 2, 1, 3)
    col_ids = jnp.arange(N_COL, dtype=jnp.int32)
    row_ids = jnp.arange(N_ROW, dtype=jnp.int32)
    running = jnp.zeros((N_COL, N_ROW, OCC_DEV, AB_DEV), jnp.float32)
    for offset in range(STEPS):
        amp_now = jnp.roll(amp_grid, offset, axis=1)
        int_now = jnp.roll(int_grid, offset, axis=0)
        block_ids = (row_ids[None, :] + col_ids[:, None] - offset) % N_COL
        factor = block_list[col_ids[:, None], block_ids].astype(jnp.float32)
        product = jnp.einsum("crok,crkn->cron", amp_now, int_now)
        running = running + factor[:, :, None, None] * product
    width = AB_DEV // N_COL
    split = running.reshape(N_COL, N_ROW, OCC_DEV, N_COL, width)
    return split.transpose(1, 3, 2, 0, 4).reshape(N_ROW * N_COL, OCC_DEV, N_COL * width)
```

```python
import functools

import jax
import jax.numpy as jnp
from jax import lax
from jax.experimental import pallas as pl
from jax.experimental.pallas import tpu as pltpu
from jax.sharding import PartitionSpec as P

GRID = ("row", "col")


def shifted(block, axis, distance):
    devices = range(lax.axis_size(axis))
    route = [((i - distance) % len(devices), i) for i in devices]
    return lax.ppermute(block, axis, route)


def shift_shards(amps, ints, block_list):
    row_pos = lax.axis_index("row")
    col_pos = lax.axis_index("col")
    col_count = lax.axis_size("col")
    running = jnp.zeros((amps.shape[0], ints.shape[1]), jnp.float32)
    held_amps = amps
    held_ints = ints
    for offset in range(col_count):
        block_id = (row_pos + col_pos - offset) % col_count
        factor = block_list[col_pos, block_id].astype(jnp.float32)
        running = running + factor * jnp.dot(
            held_amps, held_ints, preferred_element_type=jnp.float32
        )
        if offset + 1 < col_count:
            held_amps = shifted(held_amps, "row", 1)
            held_ints = shifted(held_ints, "col", 1)
    owned = lax.all_to_all(running, "col", split_axis=1, concat_axis=1, tiled=True)
    return owned.reshape(1, owned.shape[0], owned.shape[1])


def swapped(label):
    return ((label & 1) << 1) | (label >> 1)


def multiply_kernel(place, pairs, *refs, width):
    blocks, v_all, out, held, sems = refs[:16], refs[16], refs[17], refs[18], refs[19]
    row, col = place[0], place[1]
    copies = []
    for part, offset in enumerate((0, 2, 1, 3)):
        owner = col ^ offset
        held[part] = jnp.zeros(held.shape[1:], held.dtype)
        for slot in range(4):
            step = jnp.where((owner & 1) == 0, slot, swapped(slot))
            kind = ((row ^ step) + owner) & 3
            source = ((kind - row) & 3) ^ col

            @pl.when(pairs[owner, kind] != 0)
            def _(part=part, slot=slot, source=source):
                held[part] += jnp.dot(
                    blocks[part * 4 + slot][...], v_all[source], preferred_element_type=jnp.float32
                )

        start = pl.multiple_of(owner * width, width)
        copy = pltpu.make_async_copy(held.at[part], out.at[:, pl.ds(start, width)], sems.at[part])
        copy.start()
        copies.append(copy)
    for copy in copies:
        copy.wait()


def gather_shards(amps, ints, block_list):
    rows, cols = lax.axis_size("row"), lax.axis_size("col")
    row_pos, col_pos = lax.axis_index("row"), lax.axis_index("col")
    width = ints.shape[1] // cols

    def moved(block, target):
        route = [
            (r * cols + c, target(r, c)[0] * cols + target(r, c)[1])
            for r in range(rows)
            for c in range(cols)
        ]
        return lax.ppermute(block, GRID, route)

    first = functools.partial(moved, target=lambda r, c: (r ^ (1 + (c & 1)), c))
    second = functools.partial(moved, target=lambda r, c: (r ^ (2 - (c & 1)), c))
    across = functools.partial(moved, target=lambda r, c: (r, c ^ 2))
    cross = functools.partial(moved, target=lambda r, c: (r, c ^ 3))
    beside = functools.partial(moved, target=lambda r, c: (r, c ^ 1))

    def piece(offset):
        return lax.dynamic_slice_in_dim(ints, (col_pos ^ offset) * width, width, 1)

    far0 = across(amps)
    near1 = first(amps)
    near2 = second(amps)
    v2 = across(piece(2))
    v3 = cross(piece(3))
    near3 = second(near1)
    v1 = beside(piece(1))
    far1 = first(far0)
    far2 = second(far0)
    far3 = second(far1)
    own = [amps, near1, near2, near3, far0, far1, far2, far3]
    blocks = own + [beside(b) for b in own]
    v_all = jnp.stack([piece(0), v1, v2, v3])
    place = jnp.stack([row_pos, col_pos]).astype(jnp.int32)
    smem = pl.BlockSpec(memory_space=pltpu.SMEM)
    vmem = pl.BlockSpec(memory_space=pltpu.VMEM)
    out = pl.pallas_call(
        functools.partial(multiply_kernel, width=width),
        out_shape=jax.ShapeDtypeStruct((amps.shape[0], ints.shape[1]), jnp.float32),
        in_specs=[smem, smem] + [vmem] * 17,
        out_specs=pl.BlockSpec(memory_space=pl.ANY),
        scratch_shapes=[
            pltpu.VMEM((4, amps.shape[0], width), jnp.float32),
            pltpu.SemaphoreType.DMA((4,)),
        ],
        name="multiply",
    )(place, block_list, *blocks, v_all)
    return out[None]


def solution(mesh):
    placed = (P("col", "row"), P("col", "row"), P())
    whole_gather = mesh.shape["col"] == 4 and mesh.shape["row"] % 4 == 0
    return jax.shard_map(
        gather_shards if whole_gather else shift_shards,
        mesh=mesh,
        in_specs=placed,
        out_specs=P(("row", "col"), None, None),
        check_vma=False,
    )
```

```python
import functools

import jax
import jax.numpy as jnp
from jax import lax
from jax.experimental import pallas as pl
from jax.experimental.pallas import tpu as pltpu
from jax.sharding import PartitionSpec as P

GRID = ("row", "col")


def shifted(block, axis, distance):
    devices = range(lax.axis_size(axis))
    route = [((i - distance) % len(devices), i) for i in devices]
    return lax.ppermute(block, axis, route)


def shift_shards(amps, ints, block_list):
    row_pos = lax.axis_index("row")
    col_pos = lax.axis_index("col")
    col_count = lax.axis_size("col")
    running = jnp.zeros((amps.shape[0], ints.shape[1]), jnp.float32)
    held_amps = amps
    held_ints = ints
    for offset in range(col_count):
        block_id = (row_pos + col_pos - offset) % col_count
        factor = block_list[col_pos, block_id].astype(jnp.float32)
        running = running + factor * jnp.dot(
            held_amps, held_ints, preferred_element_type=jnp.float32
        )
        if offset + 1 < col_count:
            held_amps = shifted(held_amps, "row", 1)
            held_ints = shifted(held_ints, "col", 1)
    owned = lax.all_to_all(running, "col", split_axis=1, concat_axis=1, tiled=True)
    return owned.reshape(1, owned.shape[0], owned.shape[1])


def swapped(label):
    return ((label & 1) << 1) | (label >> 1)


def met_offsets(part, slot):
    met = set()
    for row in range(4):
        for col in range(4):
            owner = col ^ part
            step = swapped(slot) if owner & 1 else slot
            met.add((((row ^ step) + owner - row) & 3) ^ col)
    return sorted(met)


def multiply_kernel(pairs, *refs, parts, width):
    count = 4 * len(parts)
    blocks, pieces = refs[:count], refs[count : count + 4]
    out, sums, sems = refs[-3:]
    row, col = lax.axis_index("row"), lax.axis_index("col")
    copies = []
    for index, part in enumerate(parts):
        owner = col ^ part
        sums[index] = jnp.zeros(sums.shape[1:], sums.dtype)
        for slot in range(4):
            step = jnp.where((owner & 1) == 0, slot, swapped(slot))
            kind = ((row ^ step) + owner) & 3
            source = ((kind - row) & 3) ^ col
            listed = pairs[owner, kind] != 0
            for offset in met_offsets(part, slot):

                @pl.when(listed & (source == offset))
                def _(index=index, slot=slot, offset=offset):
                    sums[index] += jnp.dot(
                        blocks[index * 4 + slot][...],
                        pieces[offset][...],
                        preferred_element_type=jnp.float32,
                    )

        start = pl.multiple_of(owner * width, width)
        copy = pltpu.make_async_copy(
            sums.at[index], out.at[:, pl.ds(start, width)], sems.at[index]
        )
        copy.start()
        copies.append(copy)
    for copy in copies:
        copy.wait()


def multiply(block_list, blocks, pieces, parts, earlier, shape, cost):
    anywhere = pl.BlockSpec(memory_space=pl.ANY)
    vmem = pl.BlockSpec(memory_space=pltpu.VMEM)
    width = pieces[0].shape[1]
    operands = [block_list, *blocks, *pieces] + ([] if earlier is None else [earlier])
    return pl.pallas_call(
        functools.partial(multiply_kernel, parts=parts, width=width),
        out_shape=jax.ShapeDtypeStruct(shape, jnp.float32),
        in_specs=[pl.BlockSpec(memory_space=pltpu.SMEM)]
        + [vmem] * (len(blocks) + len(pieces))
        + ([] if earlier is None else [anywhere]),
        out_specs=anywhere,
        scratch_shapes=[
            pltpu.VMEM((len(parts), shape[0], width), jnp.float32),
            pltpu.SemaphoreType.DMA((len(parts),)),
        ],
        input_output_aliases={} if earlier is None else {len(operands) - 1: 0},
        cost_estimate=pl.CostEstimate(flops=cost, transcendentals=0, bytes_accessed=2**20),
        compiler_params=pltpu.CompilerParams(vmem_limit_bytes=16 * 2**20),
        name="multiply",
    )(*operands)


def after(value, *others):
    return lax.optimization_barrier((value,) + others)[0]


def gather_shards(amps, ints, block_list):
    rows, cols = lax.axis_size("row"), lax.axis_size("col")
    row_pos, col_pos = lax.axis_index("row"), lax.axis_index("col")
    width = ints.shape[1] // cols

    def moved(block, target):
        route = [
            (r * cols + c, target(r, c)[0] * cols + target(r, c)[1])
            for r in range(rows)
            for c in range(cols)
        ]
        return lax.ppermute(block, GRID, route)

    first = functools.partial(moved, target=lambda r, c: (r ^ (1 + (c & 1)), c))
    second = functools.partial(moved, target=lambda r, c: (r ^ (2 - (c & 1)), c))
    across = functools.partial(moved, target=lambda r, c: (r, c ^ 2))
    cross = functools.partial(moved, target=lambda r, c: (r, c ^ 3))
    beside = functools.partial(moved, target=lambda r, c: (r, c ^ 1))

    def piece(offset):
        return lax.dynamic_slice_in_dim(ints, (col_pos ^ offset) * width, width, 1)

    far0 = across(amps)
    near1 = first(amps)
    near2 = second(amps)
    v2 = across(after(piece(2), near1))
    v3 = cross(after(piece(3), near1))
    near3 = second(near1)
    far1 = first(far0)
    far2 = second(after(far0, near3))
    far3 = second(far1)
    pieces = [piece(0), beside(piece(1)), v2, v3]
    near = [amps, near1, near2, near3]
    far = [far0, far1, far2, far3]
    shape = (amps.shape[0], ints.shape[1])
    cost = 4 * 2 * amps.shape[0] * amps.shape[1] * width
    near += [beside(b) for b in near]
    far += [beside(b) for b in far]
    out = multiply(block_list, near, pieces, (0, 1), None, shape, 1 * cost)
    out = multiply(block_list, far, pieces, (2, 3), out, shape, cost)
    return out[None]


def solution(mesh):
    placed = (P("col", "row"), P("col", "row"), P())
    whole_gather = mesh.shape["col"] == 4 and mesh.shape["row"] % 4 == 0
    return jax.shard_map(
        gather_shards if whole_gather else shift_shards,
        mesh=mesh,
        in_specs=placed,
        out_specs=P(("row", "col"), None, None),
        check_vma=False,
    )
```

```python
import functools

import jax
import jax.numpy as jnp
from jax import lax
from jax.experimental import pallas as pl
from jax.experimental.pallas import tpu as pltpu
from jax.sharding import PartitionSpec as P

GRID = ("row", "col")


def shifted(block, axis, distance):
    devices = range(lax.axis_size(axis))
    route = [((i - distance) % len(devices), i) for i in devices]
    return lax.ppermute(block, axis, route)


def shift_shards(amps, ints, block_list):
    row_pos = lax.axis_index("row")
    col_pos = lax.axis_index("col")
    col_count = lax.axis_size("col")
    running = jnp.zeros((amps.shape[0], ints.shape[1]), jnp.float32)
    held_amps = amps
    held_ints = ints
    for offset in range(col_count):
        block_id = (row_pos + col_pos - offset) % col_count
        factor = block_list[col_pos, block_id].astype(jnp.float32)
        running = running + factor * jnp.dot(
            held_amps, held_ints, preferred_element_type=jnp.float32
        )
        if offset + 1 < col_count:
            held_amps = shifted(held_amps, "row", 1)
            held_ints = shifted(held_ints, "col", 1)
    owned = lax.all_to_all(running, "col", split_axis=1, concat_axis=1, tiled=True)
    return owned.reshape(1, owned.shape[0], owned.shape[1])


def multiply_kernel(pairs, *refs, parts, width):
    blocks, pieces, keep, send, sums = refs[:4], refs[4:6], refs[6], refs[7], refs[8]
    row, col = lax.axis_index("row"), lax.axis_index("col")
    mine = pl.multiple_of((col & 1) * width, width)
    other = pl.multiple_of(width - mine, width)
    for index, part in enumerate(parts):
        owner = col ^ part
        sums[...] = jnp.zeros(sums.shape, sums.dtype)
        for slot in range(2):
            kind = ((row ^ (2 * slot + (part & 1))) + owner) & 3
            listed = pairs[owner, kind] != 0
            here = kind == ((row + col) & 3)
            for source in range(2):
                if part & 1 == 0 and source != (slot ^ (part >> 1)):
                    continue

                @pl.when(listed & (here == (source == 0)))
                def _(slot=slot, source=source, index=index):
                    sums[...] += jnp.dot(
                        blocks[2 * index + slot][...],
                        pieces[source][...],
                        preferred_element_type=jnp.float32,
                    )

        keep[index] = sums[:, pl.ds(mine, width)]
        send[index] = sums[:, pl.ds(other, width)]


def multiply(block_list, blocks, pieces, parts, cost):
    vmem = pl.BlockSpec(memory_space=pltpu.VMEM)
    rows, width = blocks[0].shape[0], pieces[0].shape[1] // 2
    half = jax.ShapeDtypeStruct((2, rows, width), jnp.float32)
    return pl.pallas_call(
        functools.partial(multiply_kernel, parts=parts, width=width),
        out_shape=(half, half),
        in_specs=[pl.BlockSpec(memory_space=pltpu.SMEM)] + [vmem] * 6,
        out_specs=(vmem, vmem),
        scratch_shapes=[pltpu.VMEM((rows, 2 * width), jnp.float32)],
        cost_estimate=pl.CostEstimate(flops=cost, transcendentals=0, bytes_accessed=2**20),
        compiler_params=pltpu.CompilerParams(vmem_limit_bytes=8 * 2**20),
        name="multiply",
    )(block_list, *blocks, *pieces)


def add_kernel(keep, received, *refs, parts):
    out, held, sems = refs[-3:]
    col = lax.axis_index("col")
    copies = []
    for index, part in enumerate(parts):
        held[index] = keep[index] + received[1 - index]
        start = pl.multiple_of((col ^ part) * held.shape[2], held.shape[2])
        copy = pltpu.make_async_copy(
            held.at[index], out.at[:, pl.ds(start, held.shape[2])], sems.at[index]
        )
        copy.start()
        copies.append(copy)
    for copy in copies:
        copy.wait()


def add(keep, received, parts, earlier, shape):
    anywhere = pl.BlockSpec(memory_space=pl.ANY)
    vmem = pl.BlockSpec(memory_space=pltpu.VMEM)
    operands = [keep, received] + ([] if earlier is None else [earlier])
    return pl.pallas_call(
        functools.partial(add_kernel, parts=parts),
        out_shape=jax.ShapeDtypeStruct(shape, jnp.float32),
        in_specs=[vmem, vmem] + ([] if earlier is None else [anywhere]),
        out_specs=anywhere,
        scratch_shapes=[pltpu.VMEM(keep.shape, jnp.float32), pltpu.SemaphoreType.DMA((2,))],
        input_output_aliases={} if earlier is None else {2: 0},
        compiler_params=pltpu.CompilerParams(vmem_limit_bytes=8 * 2**20),
        name="add",
    )(*operands)


def gather_shards(amps, ints, block_list):
    rows, cols = lax.axis_size("row"), lax.axis_size("col")
    row_pos, col_pos = lax.axis_index("row"), lax.axis_index("col")
    width = ints.shape[1] // cols

    def moved(block, target):
        route = [
            (r * cols + c, target(r, c)[0] * cols + target(r, c)[1])
            for r in range(rows)
            for c in range(cols)
        ]
        return lax.ppermute(block, GRID, route)

    def turn(r, c):
        return (r ^ 1, c ^ 1) if (r >> 1 ^ c) & 1 else (r ^ 2, c)

    pair = functools.partial(moved, target=lambda r, c: (r ^ 2, c))
    cross = functools.partial(moved, target=lambda r, c: (r ^ 1, c ^ 1))
    across = functools.partial(moved, target=lambda r, c: (r, c ^ 2))
    beside = functools.partial(moved, target=lambda r, c: (r, c ^ 1))
    turns = ((row_pos >> 1) ^ col_pos) & 1 == 1

    def last(by_pair, by_cross):
        return moved(jnp.where(turns, by_pair, by_cross), turn)

    def chip_columns(chip):
        return lax.dynamic_slice_in_dim(ints, chip * 2 * width, 2 * width, 1)

    chip = col_pos // 2
    far0 = across(amps)
    near1 = pair(amps)
    near2 = cross(amps)
    pieces = [chip_columns(chip), across(chip_columns(1 - chip))]
    near3 = last(near1, near2)
    far1 = pair(far0)
    far2 = cross(far0)
    far3 = last(far1, far2)
    shape = (amps.shape[0], ints.shape[1])
    cost = 4 * 2 * amps.shape[0] * amps.shape[1] * width
    keep, send = multiply(block_list, [amps, near1, near2, near3], pieces, (0, 1), 30 * cost)
    out = add(keep, beside(send), (0, 1), None, shape)
    keep, send = multiply(block_list, [far0, far1, far2, far3], pieces, (2, 3), cost)
    out = add(keep, beside(send), (2, 3), out, shape)
    return out[None]


def solution(mesh):
    placed = (P("col", "row"), P("col", "row"), P())
    whole_gather = mesh.shape["col"] == 4 and mesh.shape["row"] % 4 == 0
    return jax.shard_map(
        gather_shards if whole_gather else shift_shards,
        mesh=mesh,
        in_specs=placed,
        out_specs=P(("row", "col"), None, None),
        check_vma=False,
    )
```

```python
import functools

import jax
import jax.numpy as jnp
from jax import lax
from jax.experimental import pallas as pl
from jax.experimental.pallas import tpu as pltpu
from jax.sharding import PartitionSpec as P

GRID = ("row", "col")


def shifted(block, axis, distance):
    devices = range(lax.axis_size(axis))
    route = [((i - distance) % len(devices), i) for i in devices]
    return lax.ppermute(block, axis, route)


def shift_shards(amps, ints, block_list):
    row_pos = lax.axis_index("row")
    col_pos = lax.axis_index("col")
    col_count = lax.axis_size("col")
    running = jnp.zeros((amps.shape[0], ints.shape[1]), jnp.float32)
    held_amps = amps
    held_ints = ints
    for offset in range(col_count):
        block_id = (row_pos + col_pos - offset) % col_count
        factor = block_list[col_pos, block_id].astype(jnp.float32)
        running = running + factor * jnp.dot(
            held_amps, held_ints, preferred_element_type=jnp.float32
        )
        if offset + 1 < col_count:
            held_amps = shifted(held_amps, "row", 1)
            held_ints = shifted(held_ints, "col", 1)
    owned = lax.all_to_all(running, "col", split_axis=1, concat_axis=1, tiled=True)
    return owned.reshape(1, owned.shape[0], owned.shape[1])


def multiply_kernel(pairs, *refs, parts, width):
    keep, *sends, sums = refs[-2 - len(parts) :]
    blocks = refs[: 2 * len(parts)]
    pieces = refs[2 * len(parts) : 2 * len(parts) + 2]
    row, col = lax.axis_index("row"), lax.axis_index("col")
    mine = pl.multiple_of((col & 1) * width, width)
    other = pl.multiple_of(width - mine, width)
    for index, part in enumerate(parts):
        owner = col ^ part
        sums[...] = jnp.zeros(sums.shape, sums.dtype)
        for slot in range(2):
            kind = ((row ^ (2 * slot + (part & 1))) + owner) & 3
            listed = pairs[owner, kind] != 0
            here = kind == ((row + col) & 3)
            for source in range(2):
                if part & 1 == 0 and source != (slot ^ (part >> 1)):
                    continue

                @pl.when(listed & (here == (source == 0)))
                def _(slot=slot, source=source, index=index):
                    sums[...] += jnp.dot(
                        blocks[2 * index + slot][...],
                        pieces[source][...],
                        preferred_element_type=jnp.float32,
                    )

        keep[index] = sums[:, pl.ds(mine, width)]
        sends[index][...] = sums[:, pl.ds(other, width)]


def multiply(block_list, blocks, pieces, parts, cost, ahead=()):
    vmem = pl.BlockSpec(memory_space=pltpu.VMEM)
    rows, width = blocks[0].shape[0], pieces[0].shape[1] // 2
    keep = jax.ShapeDtypeStruct((len(parts), rows, width), jnp.float32)
    send = jax.ShapeDtypeStruct((rows, width), jnp.float32)
    return pl.pallas_call(
        functools.partial(multiply_kernel, parts=parts, width=width),
        out_shape=(keep,) + (send,) * len(parts),
        in_specs=[pl.BlockSpec(memory_space=pltpu.SMEM)] + [vmem] * (len(blocks) + 2)
        + [pl.BlockSpec(memory_space=pl.ANY)] * len(ahead),
        out_specs=(vmem,) * (1 + len(parts)),
        scratch_shapes=[pltpu.VMEM((rows, 2 * width), jnp.float32)],
        cost_estimate=pl.CostEstimate(flops=cost, transcendentals=0, bytes_accessed=2**20),
        compiler_params=pltpu.CompilerParams(vmem_limit_bytes=8 * 2**20),
        name="multiply",
    )(block_list, *blocks, *pieces, *ahead)


def add_kernel(*refs, terms):
    out, held, sems = refs[-3:]
    col = lax.axis_index("col")
    width = held.shape[2]
    copies = []
    for place, (part, kept, received) in enumerate(terms):
        held[place] = refs[kept[0]][kept[1]] + refs[received][...]
        start = pl.multiple_of((col ^ part) * width, width)
        copy = pltpu.make_async_copy(
            held.at[place], out.at[:, pl.ds(start, width)], sems.at[place]
        )
        copy.start()
        copies.append(copy)
    for copy in copies:
        copy.wait()


def add(sums, terms, earlier=None):
    anywhere = pl.BlockSpec(memory_space=pl.ANY)
    vmem = pl.BlockSpec(memory_space=pltpu.VMEM)
    rows, width = sums[0].shape[1:]
    aliased = [] if earlier is None else [earlier]
    return pl.pallas_call(
        functools.partial(add_kernel, terms=terms),
        out_shape=jax.ShapeDtypeStruct((rows, 4 * width), jnp.float32),
        in_specs=[vmem] * len(sums) + [anywhere] * len(aliased),
        out_specs=anywhere,
        scratch_shapes=[
            pltpu.VMEM((len(terms), rows, width), jnp.float32),
            pltpu.SemaphoreType.DMA((len(terms),)),
        ],
        input_output_aliases={len(sums): 0} if aliased else {},
        compiler_params=pltpu.CompilerParams(vmem_limit_bytes=8 * 2**20),
        name="add",
    )(*sums, *aliased)


def gather_shards(amps, ints, block_list):
    rows, cols = lax.axis_size("row"), lax.axis_size("col")
    row_pos, col_pos = lax.axis_index("row"), lax.axis_index("col")
    width = ints.shape[1] // cols

    def moved(block, target):
        route = [
            (r * cols + c, target(r, c)[0] * cols + target(r, c)[1])
            for r in range(rows)
            for c in range(cols)
        ]
        return lax.ppermute(block, GRID, route)

    def turn(r, c):
        return (r ^ 1, c ^ 1) if (r >> 1 ^ c) & 1 else (r ^ 2, c)

    pair = functools.partial(moved, target=lambda r, c: (r ^ 2, c))
    cross = functools.partial(moved, target=lambda r, c: (r ^ 1, c ^ 1))
    across = functools.partial(moved, target=lambda r, c: (r, c ^ 2))
    beside = functools.partial(moved, target=lambda r, c: (r, c ^ 1))
    turns = ((row_pos >> 1) ^ col_pos) & 1 == 1

    def chosen(by_pair, by_cross):
        return jnp.where(turns, by_pair, by_cross)

    def chip_columns(chip):
        return lax.dynamic_slice_in_dim(ints, chip * 2 * width, 2 * width, 1)

    chip = col_pos // 2
    far0 = across(amps)
    near1 = pair(amps)
    near2 = cross(amps)
    pieces = [chip_columns(chip), across(chip_columns(1 - chip))]
    near3 = moved(chosen(near1, near2), turn)
    far1 = pair(far0)
    far2 = cross(far0)
    onward = chosen(far1, far2)
    far3 = moved(onward, turn)
    cost = 2 * 2 * amps.shape[0] * amps.shape[1] * width
    blocks = [amps, near1, near2, near3, far0, far1]
    keep, *sends = multiply(block_list, blocks, pieces, (0, 1, 2), 30 * cost, (onward,))
    received = [beside(send) for send in sends]
    last_keep, last_send = multiply(block_list, [far2, far3], pieces, (3,), cost)
    last_received = beside(last_send)
    out = add([keep, *received[:2]], ((0, (0, 0), 2), (1, (0, 1), 1)))
    sums = [keep, last_keep, received[2], last_received]
    out = add(sums, ((2, (0, 2), 3), (3, (1, 0), 2)), out)
    return out[None]


def solution(mesh):
    placed = (P("col", "row"), P("col", "row"), P())
    whole_gather = mesh.shape["col"] == 4 and mesh.shape["row"] % 4 == 0
    return jax.shard_map(
        gather_shards if whole_gather else shift_shards,
        mesh=mesh,
        in_specs=placed,
        out_specs=P(("row", "col"), None, None),
        check_vma=False,
    )
```

```python
import functools

import jax
import jax.numpy as jnp
from jax import lax
from jax.experimental import pallas as pl
from jax.experimental.pallas import tpu as pltpu
from jax.sharding import PartitionSpec as P

GRID = ("row", "col")


def shifted(block, axis, distance):
    devices = range(lax.axis_size(axis))
    route = [((i - distance) % len(devices), i) for i in devices]
    return lax.ppermute(block, axis, route)


def shift_shards(amps, ints, block_list):
    row_pos = lax.axis_index("row")
    col_pos = lax.axis_index("col")
    col_count = lax.axis_size("col")
    running = jnp.zeros((amps.shape[0], ints.shape[1]), jnp.float32)
    held_amps = amps
    held_ints = ints
    for offset in range(col_count):
        block_id = (row_pos + col_pos - offset) % col_count
        factor = block_list[col_pos, block_id].astype(jnp.float32)
        running = running + factor * jnp.dot(
            held_amps, held_ints, preferred_element_type=jnp.float32
        )
        if offset + 1 < col_count:
            held_amps = shifted(held_amps, "row", 1)
            held_ints = shifted(held_ints, "col", 1)
    owned = lax.all_to_all(running, "col", split_axis=1, concat_axis=1, tiled=True)
    return owned.reshape(1, owned.shape[0], owned.shape[1])


def multiply_kernel(pairs, *refs, groups, parts, width):
    keep, *sends, sums = refs[-2 - len(parts) :]
    refs = list(refs)
    blocks = [[refs.pop(0) if used else None for used in group] for group in groups]
    pieces = refs[:2]
    row, col = lax.axis_index("row"), lax.axis_index("col")
    mine = pl.multiple_of((col & 1) * width, width)
    other = pl.multiple_of(width - mine, width)
    turned = (((row >> 1) ^ col) & 1) == 1
    for index, part in enumerate(parts):
        owner = col ^ part
        sums[...] = jnp.zeros(sums.shape, sums.dtype)
        if part & 1 == 0:
            choices = ((0, 0, None), (1, 1, True), (1, 2, False))
        else:
            choices = ((0, 1, False), (0, 2, True), (1, 3, None))
        for slot, label, when_turned in choices:
            block = blocks[index][label]
            kind = ((row ^ (2 * slot + (part & 1))) + owner) & 3
            listed = pairs[owner, kind] != 0
            if when_turned is not None:
                listed = listed & (turned if when_turned else ~turned)
            here = kind == ((row + col) & 3)
            for source in range(2):
                if part & 1 == 0 and source != (slot ^ (part >> 1)):
                    continue

                @pl.when(listed & (here == (source == 0)))
                def _(block=block, source=source):
                    sums[...] += jnp.dot(
                        block[...], pieces[source][...], preferred_element_type=jnp.float32
                    )

        keep[index] = sums[:, pl.ds(mine, width)]
        sends[index][...] = sums[:, pl.ds(other, width)]


def multiply(block_list, groups, pieces, parts, cost):
    vmem = pl.BlockSpec(memory_space=pltpu.VMEM)
    blocks = [block for group in groups for block in group if block is not None]
    rows, width = blocks[0].shape[0], pieces[0].shape[1] // 2
    keep = jax.ShapeDtypeStruct((len(parts), rows, width), jnp.float32)
    send = jax.ShapeDtypeStruct((rows, width), jnp.float32)
    used = tuple(tuple(block is not None for block in group) for group in groups)
    return pl.pallas_call(
        functools.partial(multiply_kernel, groups=used, parts=parts, width=width),
        out_shape=(keep,) + (send,) * len(parts),
        in_specs=[pl.BlockSpec(memory_space=pltpu.SMEM)] + [vmem] * (len(blocks) + 2),
        out_specs=(vmem,) * (1 + len(parts)),
        scratch_shapes=[pltpu.VMEM((rows, 2 * width), jnp.float32)],
        cost_estimate=pl.CostEstimate(flops=cost, transcendentals=0, bytes_accessed=2**20),
        compiler_params=pltpu.CompilerParams(vmem_limit_bytes=8 * 2**20),
        name="multiply",
    )(block_list, *blocks, *pieces)


def add_kernel(*refs, terms):
    out, held, sems = refs[-3:]
    col = lax.axis_index("col")
    width = held.shape[2]
    copies = []
    for place, (part, kept, received) in enumerate(terms):
        held[place] = refs[kept[0]][kept[1]] + refs[received][...]
        start = pl.multiple_of((col ^ part) * width, width)
        copy = pltpu.make_async_copy(
            held.at[place], out.at[:, pl.ds(start, width)], sems.at[place]
        )
        copy.start()
        copies.append(copy)
    for copy in copies:
        copy.wait()


def add(sums, terms, earlier=None):
    anywhere = pl.BlockSpec(memory_space=pl.ANY)
    vmem = pl.BlockSpec(memory_space=pltpu.VMEM)
    rows, width = sums[0].shape[1:]
    aliased = [] if earlier is None else [earlier]
    return pl.pallas_call(
        functools.partial(add_kernel, terms=terms),
        out_shape=jax.ShapeDtypeStruct((rows, 4 * width), jnp.float32),
        in_specs=[vmem] * len(sums) + [anywhere] * len(aliased),
        out_specs=anywhere,
        scratch_shapes=[
            pltpu.VMEM((len(terms), rows, width), jnp.float32),
            pltpu.SemaphoreType.DMA((len(terms),)),
        ],
        input_output_aliases={len(sums): 0} if aliased else {},
        compiler_params=pltpu.CompilerParams(vmem_limit_bytes=8 * 2**20),
        name="add",
    )(*sums, *aliased)


def gather_shards(amps, ints, block_list):
    rows, cols = lax.axis_size("row"), lax.axis_size("col")
    col_pos = lax.axis_index("col")
    width = ints.shape[1] // cols

    def moved(block, target):
        route = [
            (r * cols + c, target(r, c)[0] * cols + target(r, c)[1])
            for r in range(rows)
            for c in range(cols)
        ]
        return lax.ppermute(block, GRID, route)

    def either(flip):
        return lambda r, c: (r ^ 1, c ^ 1) if (r >> 1 ^ c ^ flip) & 1 else (r ^ 2, c)

    first = functools.partial(moved, target=either(0))
    second = functools.partial(moved, target=either(1))
    across = functools.partial(moved, target=lambda r, c: (r, c ^ 2))
    beside = functools.partial(moved, target=lambda r, c: (r, c ^ 1))

    def chip_columns(chip):
        return lax.dynamic_slice_in_dim(ints, chip * 2 * width, 2 * width, 1)

    chip = col_pos // 2
    far0 = across(amps)
    near1 = first(amps)
    near2 = second(amps)
    pieces = [chip_columns(chip), across(chip_columns(1 - chip))]
    far0, near2 = lax.optimization_barrier((far0, near2))
    near3 = first(near1)
    far1 = first(far0)
    far2 = second(far0)
    far3 = first(far1)
    cost = 2 * 2 * amps.shape[0] * amps.shape[1] * width
    run = functools.partial(multiply, block_list, pieces=pieces)
    groups = [[amps, near1, near2, None], [far0, far1, far2, None]]
    keep, *sends = run(groups=groups, parts=(0, 2), cost=15 * cost)
    received0, received2 = [beside(send) for send in sends]
    keep1, send1 = run(groups=[[None, near1, near2, near3]], parts=(1,), cost=15 * cost)
    received1 = beside(send1)
    keep3, send3 = run(groups=[[None, far1, far2, far3]], parts=(3,), cost=cost)
    received3 = beside(send3)
    out = add([keep, keep1, received0, received1], ((0, (0, 0), 3), (1, (1, 0), 2)))
    out = add([keep, keep3, received2, received3], ((2, (0, 1), 3), (3, (1, 0), 2)), out)
    return out[None]


def solution(mesh):
    placed = (P("col", "row"), P("col", "row"), P())
    whole_gather = mesh.shape["col"] == 4 and mesh.shape["row"] % 4 == 0
    return jax.shard_map(
        gather_shards if whole_gather else shift_shards,
        mesh=mesh,
        in_specs=placed,
        out_specs=P(("row", "col"), None, None),
        check_vma=False,
    )
```

```python
import functools

import jax
import jax.numpy as jnp
from jax import lax
from jax.experimental import pallas as pl
from jax.experimental.pallas import tpu as pltpu
from jax.sharding import PartitionSpec as P

GRID = ("row", "col")


def shifted(block, axis, distance):
    devices = range(lax.axis_size(axis))
    route = [((i - distance) % len(devices), i) for i in devices]
    return lax.ppermute(block, axis, route)


def shift_shards(amps, ints, block_list):
    row_pos = lax.axis_index("row")
    col_pos = lax.axis_index("col")
    col_count = lax.axis_size("col")
    running = jnp.zeros((amps.shape[0], ints.shape[1]), jnp.float32)
    held_amps = amps
    held_ints = ints
    for offset in range(col_count):
        block_id = (row_pos + col_pos - offset) % col_count
        factor = block_list[col_pos, block_id].astype(jnp.float32)
        running = running + factor * jnp.dot(
            held_amps, held_ints, preferred_element_type=jnp.float32
        )
        if offset + 1 < col_count:
            held_amps = shifted(held_amps, "row", 1)
            held_ints = shifted(held_ints, "col", 1)
    owned = lax.all_to_all(running, "col", split_axis=1, concat_axis=1, tiled=True)
    return owned.reshape(1, owned.shape[0], owned.shape[1])


def multiply_kernel(pairs, *refs, groups, parts, width):
    keep, send, sums = refs[-3:]
    refs = list(refs)
    blocks = [[refs.pop(0) if used else None for used in group] for group in groups]
    pieces = refs[:2]
    row, col = lax.axis_index("row"), lax.axis_index("col")
    bit = lax.broadcasted_iota(jnp.int32, pairs.shape, 0) * 4
    bit = bit + lax.broadcasted_iota(jnp.int32, pairs.shape, 1)
    table = jnp.where(pairs[...] != 0, jnp.left_shift(1, bit), 0)
    table = jnp.sum(table.astype(jnp.float32)).astype(jnp.int32)
    mine = pl.multiple_of((col & 1) * width, width)
    other = pl.multiple_of(width - mine, width)
    turned = (((row >> 1) ^ col) & 1) == 1
    for index, part in enumerate(parts):
        owner = col ^ part
        sums[...] = jnp.zeros(sums.shape, sums.dtype)
        if part & 1 == 0:
            choices = ((0, 0, None), (1, 1, True), (1, 2, False))
        else:
            choices = ((0, 1, False), (0, 2, True), (1, 3, None))
        for slot, label, when_turned in choices:
            block = blocks[index][label]
            kind = ((row ^ (2 * slot + (part & 1))) + owner) & 3
            listed = (lax.shift_right_logical(table, owner * 4 + kind) & 1) == 1
            if when_turned is not None:
                listed = listed & (turned if when_turned else ~turned)
            here = kind == ((row + col) & 3)
            for source in range(2):
                if part & 1 == 0 and source != (slot ^ (part >> 1)):
                    continue

                @pl.when(listed & (here == (source == 0)))
                def _(block=block, source=source):
                    sums[...] += jnp.dot(
                        block[...], pieces[source][...], preferred_element_type=jnp.float32
                    )

        keep[index] = sums[:, pl.ds(mine, width)]
        send[index] = sums[:, pl.ds(other, width)]


def multiply(block_list, groups, pieces, parts, cost):
    vmem = pl.BlockSpec(memory_space=pltpu.VMEM)
    blocks = [block for group in groups for block in group if block is not None]
    rows, width = blocks[0].shape[0], pieces[0].shape[1] // 2
    keep = jax.ShapeDtypeStruct((len(parts), rows, width), jnp.float32)
    used = tuple(tuple(block is not None for block in group) for group in groups)
    return pl.pallas_call(
        functools.partial(multiply_kernel, groups=used, parts=parts, width=width),
        out_shape=(keep, keep),
        in_specs=[vmem] * (len(blocks) + 3),
        out_specs=(vmem, vmem),
        scratch_shapes=[pltpu.VMEM((rows, 2 * width), jnp.float32)],
        cost_estimate=pl.CostEstimate(flops=cost, transcendentals=0, bytes_accessed=2**20),
        compiler_params=pltpu.CompilerParams(vmem_limit_bytes=8 * 2**20),
        name="multiply",
    )(block_list, *blocks, *pieces)


def add_kernel(*refs, terms):
    out, held, sems = refs[-3:]
    col = lax.axis_index("col")
    width = held.shape[2]
    copies = []
    for place, (part, kept, received) in enumerate(terms):
        held[place] = refs[kept[0]][kept[1]] + refs[received[0]][received[1]]
        start = pl.multiple_of((col ^ part) * width, width)
        copy = pltpu.make_async_copy(
            held.at[place], out.at[:, pl.ds(start, width)], sems.at[place]
        )
        copy.start()
        copies.append(copy)
    for copy in copies:
        copy.wait()


def add(sums, terms, earlier=None):
    anywhere = pl.BlockSpec(memory_space=pl.ANY)
    vmem = pl.BlockSpec(memory_space=pltpu.VMEM)
    rows, width = sums[0].shape[1:]
    aliased = [] if earlier is None else [earlier]
    return pl.pallas_call(
        functools.partial(add_kernel, terms=terms),
        out_shape=jax.ShapeDtypeStruct((rows, 4 * width), jnp.float32),
        in_specs=[vmem] * len(sums) + [anywhere] * len(aliased),
        out_specs=anywhere,
        scratch_shapes=[
            pltpu.VMEM((len(terms), rows, width), jnp.float32),
            pltpu.SemaphoreType.DMA((len(terms),)),
        ],
        input_output_aliases={len(sums): 0} if aliased else {},
        compiler_params=pltpu.CompilerParams(vmem_limit_bytes=8 * 2**20),
        name="add",
    )(*sums, *aliased)


def gather_shards(amps, ints, block_list):
    rows, cols = lax.axis_size("row"), lax.axis_size("col")
    col_pos = lax.axis_index("col")
    width = ints.shape[1] // cols

    def moved(block, target):
        route = [
            (r * cols + c, target(r, c)[0] * cols + target(r, c)[1])
            for r in range(rows)
            for c in range(cols)
        ]
        return lax.ppermute(block, GRID, route)

    def either(flip):
        return lambda r, c: (r ^ 1, c ^ 1) if (r >> 1 ^ c ^ flip) & 1 else (r ^ 2, c)

    first = functools.partial(moved, target=either(0))
    second = functools.partial(moved, target=either(1))
    across = functools.partial(moved, target=lambda r, c: (r, c ^ 2))
    beside = functools.partial(moved, target=lambda r, c: (r, c ^ 1))

    def chip_columns(chip):
        return lax.dynamic_slice_in_dim(ints, chip * 2 * width, 2 * width, 1)

    chip = col_pos // 2
    far0 = across(amps)
    near1 = first(amps)
    near2 = second(amps)
    pieces = [chip_columns(chip), across(chip_columns(1 - chip))]
    far0, near2 = lax.optimization_barrier((far0, near2))
    near3 = first(near1)
    far1 = first(far0)
    far2 = second(far0)
    far3 = first(far1)
    cost = 2 * 2 * amps.shape[0] * amps.shape[1] * width
    run = functools.partial(multiply, block_list, pieces=pieces)
    groups = [[amps, near1, near2, None], [far0, far1, far2, None]]
    keep, send = run(groups=groups, parts=(0, 2), cost=15 * cost)
    received = beside(send)
    keep1, send1 = run(groups=[[None, near1, near2, near3]], parts=(1,), cost=15 * cost)
    received1 = beside(send1)
    keep3, send3 = run(groups=[[None, far1, far2, far3]], parts=(3,), cost=cost)
    received3 = beside(send3)
    out = add([keep, keep1, received, received1], ((0, (0, 0), (3, 0)), (1, (1, 0), (2, 0))))
    out = add([keep, keep3, received, received3], ((2, (0, 1), (3, 0)), (3, (1, 0), (2, 1))), out)
    return out[None]


def solution(mesh):
    placed = (P("col", "row"), P("col", "row"), P())
    whole_gather = mesh.shape["col"] == 4 and mesh.shape["row"] % 4 == 0
    return jax.shard_map(
        gather_shards if whole_gather else shift_shards,
        mesh=mesh,
        in_specs=placed,
        out_specs=P(("row", "col"), None, None),
        check_vma=False,
    )
```

```python
import functools

import jax
import jax.numpy as jnp
from jax import lax
from jax.experimental import pallas as pl
from jax.experimental.pallas import tpu as pltpu
from jax.sharding import PartitionSpec as P

GRID = ("row", "col")


def shifted(block, axis, distance):
    devices = range(lax.axis_size(axis))
    route = [((i - distance) % len(devices), i) for i in devices]
    return lax.ppermute(block, axis, route)


def shift_shards(amps, ints, block_list):
    row_pos = lax.axis_index("row")
    col_pos = lax.axis_index("col")
    col_count = lax.axis_size("col")
    running = jnp.zeros((amps.shape[0], ints.shape[1]), jnp.float32)
    held_amps = amps
    held_ints = ints
    for offset in range(col_count):
        block_id = (row_pos + col_pos - offset) % col_count
        factor = block_list[col_pos, block_id].astype(jnp.float32)
        running = running + factor * jnp.dot(
            held_amps, held_ints, preferred_element_type=jnp.float32
        )
        if offset + 1 < col_count:
            held_amps = shifted(held_amps, "row", 1)
            held_ints = shifted(held_ints, "col", 1)
    owned = lax.all_to_all(running, "col", split_axis=1, concat_axis=1, tiled=True)
    return owned.reshape(1, owned.shape[0], owned.shape[1])


def multiply_kernel(pairs, *refs, groups, parts, opening, begun, width):
    refs = list(refs)
    blocks = [[refs.pop(0) if used else None for used in group] for group in groups]
    pieces, refs = refs[:2], refs[2:]
    started = refs.pop(0) if begun else None
    keep, send, *opened, sums = refs
    row, col = lax.axis_index("row"), lax.axis_index("col")
    bit = lax.broadcasted_iota(jnp.int32, pairs.shape, 0) * 4
    bit = bit + lax.broadcasted_iota(jnp.int32, pairs.shape, 1)
    table = jnp.where(pairs[...] != 0, jnp.left_shift(1, bit), 0)
    table = jnp.sum(table.astype(jnp.float32)).astype(jnp.int32)
    mine = pl.multiple_of((col & 1) * width, width)
    other = pl.multiple_of(width - mine, width)
    turned = (((row >> 1) ^ col) & 1) == 1
    for index, part in enumerate(parts + opening):
        owner = col ^ part
        total = sums if index < len(parts) else opened[0]
        if begun and index == 0:
            total[...] = started[...]
        else:
            total[...] = jnp.zeros(total.shape, total.dtype)
        if part & 1 == 0:
            choices = ((0, 0, None), (1, 1, True), (1, 2, False))
        else:
            choices = ((0, 1, False), (0, 2, True), (1, 3, None))
        for slot, label, when_turned in choices:
            block = blocks[index][label]
            if block is None:
                continue
            kind = ((row ^ (2 * slot + (part & 1))) + owner) & 3
            listed = (lax.shift_right_logical(table, owner * 4 + kind) & 1) == 1
            if when_turned is not None:
                listed = listed & (turned if when_turned else ~turned)
            here = kind == ((row + col) & 3)
            for source in range(2):
                if part & 1 == 0 and source != (slot ^ (part >> 1)):
                    continue

                @pl.when(listed & (here == (source == 0)))
                def _(block=block, source=source, total=total):
                    total[...] += jnp.dot(
                        block[...], pieces[source][...], preferred_element_type=jnp.float32
                    )

        if index < len(parts):
            keep[index] = sums[:, pl.ds(mine, width)]
            send[index] = sums[:, pl.ds(other, width)]


def multiply(block_list, groups, pieces, parts, cost, opening=(), begun=None):
    vmem = pl.BlockSpec(memory_space=pltpu.VMEM)
    blocks = [block for group in groups for block in group if block is not None]
    operands = [block_list, *blocks, *pieces] + ([] if begun is None else [begun])
    rows, width = blocks[0].shape[0], pieces[0].shape[1] // 2
    keep = jax.ShapeDtypeStruct((len(parts), rows, width), jnp.float32)
    full = jax.ShapeDtypeStruct((rows, 2 * width), jnp.float32)
    used = tuple(tuple(block is not None for block in group) for group in groups)
    return pl.pallas_call(
        functools.partial(
            multiply_kernel,
            groups=used,
            parts=parts,
            opening=opening,
            begun=begun is not None,
            width=width,
        ),
        out_shape=(keep, keep) + (full,) * len(opening),
        in_specs=[vmem] * len(operands),
        out_specs=(vmem,) * (2 + len(opening)),
        scratch_shapes=[pltpu.VMEM(full.shape, full.dtype)],
        cost_estimate=pl.CostEstimate(flops=cost, transcendentals=0, bytes_accessed=2**20),
        compiler_params=pltpu.CompilerParams(vmem_limit_bytes=8 * 2**20),
        name="multiply",
    )(*operands)


def add_kernel(*refs, terms):
    out, held, sems = refs[-3:]
    col = lax.axis_index("col")
    width = held.shape[2]
    copies = []
    for place, (part, kept, received) in enumerate(terms):
        held[place] = refs[kept[0]][kept[1]] + refs[received[0]][received[1]]
        start = pl.multiple_of((col ^ part) * width, width)
        copy = pltpu.make_async_copy(
            held.at[place], out.at[:, pl.ds(start, width)], sems.at[place]
        )
        copy.start()
        copies.append(copy)
    for copy in copies:
        copy.wait()


def add(sums, terms, earlier=None):
    anywhere = pl.BlockSpec(memory_space=pl.ANY)
    vmem = pl.BlockSpec(memory_space=pltpu.VMEM)
    rows, width = sums[0].shape[1:]
    aliased = [] if earlier is None else [earlier]
    return pl.pallas_call(
        functools.partial(add_kernel, terms=terms),
        out_shape=jax.ShapeDtypeStruct((rows, 4 * width), jnp.float32),
        in_specs=[vmem] * len(sums) + [anywhere] * len(aliased),
        out_specs=anywhere,
        scratch_shapes=[
            pltpu.VMEM((len(terms), rows, width), jnp.float32),
            pltpu.SemaphoreType.DMA((len(terms),)),
        ],
        input_output_aliases={len(sums): 0} if aliased else {},
        compiler_params=pltpu.CompilerParams(vmem_limit_bytes=8 * 2**20),
        name="add",
    )(*sums, *aliased)


def gather_shards(amps, ints, block_list):
    rows, cols = lax.axis_size("row"), lax.axis_size("col")
    col_pos = lax.axis_index("col")
    width = ints.shape[1] // cols

    def moved(block, target):
        route = [
            (r * cols + c, target(r, c)[0] * cols + target(r, c)[1])
            for r in range(rows)
            for c in range(cols)
        ]
        return lax.ppermute(block, GRID, route)

    def either(flip):
        return lambda r, c: (r ^ 1, c ^ 1) if (r >> 1 ^ c ^ flip) & 1 else (r ^ 2, c)

    first = functools.partial(moved, target=either(0))
    second = functools.partial(moved, target=either(1))
    across = functools.partial(moved, target=lambda r, c: (r, c ^ 2))
    beside = functools.partial(moved, target=lambda r, c: (r, c ^ 1))

    def chip_columns(chip):
        return lax.dynamic_slice_in_dim(ints, chip * 2 * width, 2 * width, 1)

    chip = col_pos // 2
    far0 = across(amps)
    near1 = first(amps)
    near2 = second(amps)
    pieces = [chip_columns(chip), across(chip_columns(1 - chip))]
    far0, near2 = lax.optimization_barrier((far0, near2))
    near3 = first(near1)
    far1 = first(far0)
    far2 = second(far0)
    far3 = first(far1)
    cost = 2 * 2 * amps.shape[0] * amps.shape[1] * width
    run = functools.partial(multiply, block_list, pieces=pieces)
    groups = [[amps, near1, near2, None], [far0, far1, far2, None]]
    keep, send = run(groups=groups, parts=(0, 2), cost=15 * cost)
    received = beside(send)
    groups = [[None, near1, near2, near3], [None, far1, far2, None]]
    keep1, send1, begun = run(groups=groups, parts=(1,), cost=15 * cost, opening=(3,))
    received1 = beside(send1)
    groups = [[None, None, None, far3]]
    keep3, send3 = run(groups=groups, parts=(3,), cost=cost, begun=begun)
    received3 = beside(send3)
    sums = [keep, keep1, keep3, received, received1]
    out = add(sums, ((0, (0, 0), (4, 0)), (1, (1, 0), (3, 0)), (3, (2, 0), (3, 1))))
    out = add([keep, received3], ((2, (0, 1), (1, 0)),), out)
    return out[None]


def solution(mesh):
    placed = (P("col", "row"), P("col", "row"), P())
    whole_gather = mesh.shape["col"] == 4 and mesh.shape["row"] % 4 == 0
    return jax.shard_map(
        gather_shards if whole_gather else shift_shards,
        mesh=mesh,
        in_specs=placed,
        out_specs=P(("row", "col"), None, None),
        check_vma=False,
    )
```

```python
import functools

import jax
import jax.numpy as jnp
from jax import lax
from jax.experimental import pallas as pl
from jax.experimental.pallas import tpu as pltpu
from jax.sharding import PartitionSpec as P

GRID = ("row", "col")


def shifted(block, axis, distance):
    devices = range(lax.axis_size(axis))
    route = [((i - distance) % len(devices), i) for i in devices]
    return lax.ppermute(block, axis, route)


def shift_shards(amps, ints, block_list):
    row_pos = lax.axis_index("row")
    col_pos = lax.axis_index("col")
    col_count = lax.axis_size("col")
    running = jnp.zeros((amps.shape[0], ints.shape[1]), jnp.float32)
    held_amps = amps
    held_ints = ints
    for offset in range(col_count):
        block_id = (row_pos + col_pos - offset) % col_count
        factor = block_list[col_pos, block_id].astype(jnp.float32)
        running = running + factor * jnp.dot(
            held_amps, held_ints, preferred_element_type=jnp.float32
        )
        if offset + 1 < col_count:
            held_amps = shifted(held_amps, "row", 1)
            held_ints = shifted(held_ints, "col", 1)
    owned = lax.all_to_all(running, "col", split_axis=1, concat_axis=1, tiled=True)
    return owned.reshape(1, owned.shape[0], owned.shape[1])


def multiply_kernel(pairs, *refs, groups, parts, opening, begun, width):
    refs = list(refs)
    blocks = [[refs.pop(0) if used else None for used in group] for group in groups]
    pieces, refs = refs[:2], refs[2:]
    started = refs.pop(0) if begun else None
    keep, send, *opened, sums = refs
    row, col = lax.axis_index("row"), lax.axis_index("col")
    bit = lax.broadcasted_iota(jnp.int32, pairs.shape, 0) * 4
    bit = bit + lax.broadcasted_iota(jnp.int32, pairs.shape, 1)
    table = jnp.where(pairs[...] != 0, jnp.left_shift(1, bit), 0)
    table = jnp.sum(table.astype(jnp.float32)).astype(jnp.int32)
    mine = pl.multiple_of((col & 1) * width, width)
    other = pl.multiple_of(width - mine, width)
    turned = (((row >> 1) ^ col) & 1) == 1
    for index, part in enumerate(parts + opening):
        owner = col ^ part
        total = sums if index < len(parts) else opened[0]
        if begun and index == 0:
            total[...] = started[...]
        else:
            total[...] = jnp.zeros(total.shape, total.dtype)
        if part & 1 == 0:
            choices = ((0, 0, None), (1, 1, True), (1, 2, False))
        else:
            choices = ((0, 1, False), (0, 2, True), (1, 3, None))
        for slot, label, when_turned in choices:
            block = blocks[index][label]
            if block is None:
                continue
            kind = ((row ^ (2 * slot + (part & 1))) + owner) & 3
            listed = (lax.shift_right_logical(table, owner * 4 + kind) & 1) == 1
            if when_turned is not None:
                listed = listed & (turned if when_turned else ~turned)
            here = kind == ((row + col) & 3)
            for source in range(2):
                if part & 1 == 0 and source != (slot ^ (part >> 1)):
                    continue

                @pl.when(listed & (here == (source == 0)))
                def _(block=block, source=source, total=total):
                    total[...] += jnp.dot(
                        block[...], pieces[source][...], preferred_element_type=jnp.float32
                    )

        if index < len(parts):
            keep[index] = sums[:, pl.ds(mine, width)]
            send[index] = sums[:, pl.ds(other, width)]


def multiply(block_list, groups, pieces, parts, cost, opening=(), begun=None):
    vmem = pl.BlockSpec(memory_space=pltpu.VMEM)
    blocks = [block for group in groups for block in group if block is not None]
    operands = [block_list, *blocks, *pieces] + ([] if begun is None else [begun])
    rows, width = blocks[0].shape[0], pieces[0].shape[1] // 2
    keep = jax.ShapeDtypeStruct((len(parts), rows, width), jnp.float32)
    full = jax.ShapeDtypeStruct((rows, 2 * width), jnp.float32)
    used = tuple(tuple(block is not None for block in group) for group in groups)
    return pl.pallas_call(
        functools.partial(
            multiply_kernel,
            groups=used,
            parts=parts,
            opening=opening,
            begun=begun is not None,
            width=width,
        ),
        out_shape=(keep, keep) + (full,) * len(opening),
        in_specs=[vmem] * len(operands),
        out_specs=(vmem,) * (2 + len(opening)),
        scratch_shapes=[pltpu.VMEM(full.shape, full.dtype)],
        cost_estimate=pl.CostEstimate(flops=cost, transcendentals=0, bytes_accessed=2**20),
        compiler_params=pltpu.CompilerParams(vmem_limit_bytes=8 * 2**20),
        name="multiply",
    )(*operands)


def add_kernel(*refs, terms):
    out, held, sems = refs[-3:]
    col = lax.axis_index("col")
    width = held.shape[2]
    copies = []
    for place, (part, kept, received) in enumerate(terms):
        held[place] = refs[kept[0]][kept[1]] + refs[received[0]][received[1]]
        start = pl.multiple_of((col ^ part) * width, width)
        copy = pltpu.make_async_copy(
            held.at[place], out.at[:, pl.ds(start, width)], sems.at[place]
        )
        copy.start()
        copies.append(copy)
    for copy in copies:
        copy.wait()


def add(sums, terms, earlier=None):
    anywhere = pl.BlockSpec(memory_space=pl.ANY)
    vmem = pl.BlockSpec(memory_space=pltpu.VMEM)
    rows, width = sums[0].shape[1:]
    aliased = [] if earlier is None else [earlier]
    return pl.pallas_call(
        functools.partial(add_kernel, terms=terms),
        out_shape=jax.ShapeDtypeStruct((rows, 4 * width), jnp.float32),
        in_specs=[vmem] * len(sums) + [anywhere] * len(aliased),
        out_specs=anywhere,
        scratch_shapes=[
            pltpu.VMEM((len(terms), rows, width), jnp.float32),
            pltpu.SemaphoreType.DMA((len(terms),)),
        ],
        input_output_aliases={len(sums): 0} if aliased else {},
        compiler_params=pltpu.CompilerParams(vmem_limit_bytes=8 * 2**20),
        name="add",
    )(*sums, *aliased)


def gather_shards(amps, ints, block_list):
    rows, cols = lax.axis_size("row"), lax.axis_size("col")
    col_pos = lax.axis_index("col")
    width = ints.shape[1] // cols

    def moved(block, target):
        route = [
            (r * cols + c, target(r, c)[0] * cols + target(r, c)[1])
            for r in range(rows)
            for c in range(cols)
        ]
        return lax.ppermute(block, GRID, route)

    def either(flip):
        return lambda r, c: (r ^ 1, c ^ 1) if (r >> 1 ^ c ^ flip) & 1 else (r ^ 2, c)

    first = functools.partial(moved, target=either(0))
    second = functools.partial(moved, target=either(1))
    across = functools.partial(moved, target=lambda r, c: (r, c ^ 2))
    beside = functools.partial(moved, target=lambda r, c: (r, c ^ 1))

    def chip_columns(chip):
        return lax.dynamic_slice_in_dim(ints, chip * 2 * width, 2 * width, 1)

    chip = col_pos // 2
    far0 = across(amps)
    near1 = first(amps)
    near2 = second(amps)
    pieces = [chip_columns(chip), across(chip_columns(1 - chip))]
    far0, near2 = lax.optimization_barrier((far0, near2))
    near3 = first(near1)
    far1 = first(far0)
    far2 = second(far0)
    far3 = first(far1)
    cost = 2 * 2 * amps.shape[0] * amps.shape[1] * width
    run = functools.partial(multiply, block_list, pieces=pieces)
    groups = [[amps, near1, near2, None], [far0, far1, far2, None]]
    keep, send = run(groups=groups, parts=(0, 2), cost=2 * cost)
    received = beside(send)
    groups = [[None, near1, near2, near3], [None, far1, far2, None]]
    keep1, send1, begun = run(groups=groups, parts=(1,), cost=cost, opening=(3,))
    received1 = beside(send1)
    groups = [[None, None, None, far3]]
    keep3, send3 = run(groups=groups, parts=(3,), cost=cost, begun=begun)
    received3 = beside(send3)
    sums = [keep, keep1, keep3, received, received1]
    out = add(sums, ((0, (0, 0), (4, 0)), (1, (1, 0), (3, 0)), (3, (2, 0), (3, 1))))
    out = add([keep, received3], ((2, (0, 1), (1, 0)),), out)
    return out[None]


def solution(mesh):
    placed = (P("col", "row"), P("col", "row"), P())
    whole_gather = mesh.shape["col"] == 4 and mesh.shape["row"] % 4 == 0
    return jax.shard_map(
        gather_shards if whole_gather else shift_shards,
        mesh=mesh,
        in_specs=placed,
        out_specs=P(("row", "col"), None, None),
        check_vma=False,
    )
```

```python
import functools

import jax
import jax.numpy as jnp
from jax import lax
from jax.experimental import pallas as pl
from jax.experimental.pallas import tpu as pltpu
from jax.sharding import PartitionSpec as P

GRID = ("row", "col")


def shifted(block, axis, distance):
    devices = range(lax.axis_size(axis))
    route = [((i - distance) % len(devices), i) for i in devices]
    return lax.ppermute(block, axis, route)


def shift_shards(amps, ints, block_list):
    row_pos = lax.axis_index("row")
    col_pos = lax.axis_index("col")
    col_count = lax.axis_size("col")
    running = jnp.zeros((amps.shape[0], ints.shape[1]), jnp.float32)
    held_amps = amps
    held_ints = ints
    for offset in range(col_count):
        block_id = (row_pos + col_pos - offset) % col_count
        factor = block_list[col_pos, block_id].astype(jnp.float32)
        running = running + factor * jnp.dot(
            held_amps, held_ints, preferred_element_type=jnp.float32
        )
        if offset + 1 < col_count:
            held_amps = shifted(held_amps, "row", 1)
            held_ints = shifted(held_ints, "col", 1)
    owned = lax.all_to_all(running, "col", split_axis=1, concat_axis=1, tiled=True)
    return owned.reshape(1, owned.shape[0], owned.shape[1])


def multiply_kernel(pairs, *refs, groups, parts, opening, begun, width):
    refs = list(refs)
    blocks = [[refs.pop(0) if used else None for used in group] for group in groups]
    pieces, refs = refs[:2], refs[2:]
    started = refs.pop(0) if begun else None
    keep, send, *opened, sums = refs
    row, col = lax.axis_index("row"), lax.axis_index("col")
    bit = lax.broadcasted_iota(jnp.int32, pairs.shape, 0) * 4
    bit = bit + lax.broadcasted_iota(jnp.int32, pairs.shape, 1)
    table = jnp.where(pairs[...] != 0, jnp.left_shift(1, bit), 0)
    table = jnp.sum(table.astype(jnp.float32)).astype(jnp.int32)
    mine = pl.multiple_of((col & 1) * width, width)
    other = pl.multiple_of(width - mine, width)
    turned = (((row >> 1) ^ col) & 1) == 1
    for index, part in enumerate(parts + opening):
        owner = col ^ part
        total = sums if index < len(parts) else opened[0]
        if begun and index == 0:
            total[...] = started[...]
        else:
            total[...] = jnp.zeros(total.shape, total.dtype)
        if part & 1 == 0:
            choices = ((0, 0, None), (1, 1, True), (1, 2, False))
        else:
            choices = ((0, 1, False), (0, 2, True), (1, 3, None))
        for slot, label, when_turned in choices:
            block = blocks[index][label]
            if block is None:
                continue
            kind = ((row ^ (2 * slot + (part & 1))) + owner) & 3
            listed = (lax.shift_right_logical(table, owner * 4 + kind) & 1) == 1
            if when_turned is not None:
                listed = listed & (turned if when_turned else ~turned)
            here = kind == ((row + col) & 3)
            for source in range(2):
                if part & 1 == 0 and source != (slot ^ (part >> 1)):
                    continue

                @pl.when(listed & (here == (source == 0)))
                def _(block=block, source=source, total=total):
                    total[...] += jnp.dot(
                        block[...], pieces[source][...], preferred_element_type=jnp.float32
                    )

        if index < len(parts):
            keep[index] = sums[:, pl.ds(mine, width)]
            send[index] = sums[:, pl.ds(other, width)]


def multiply(block_list, groups, pieces, parts, cost, opening=(), begun=None):
    vmem = pl.BlockSpec(memory_space=pltpu.VMEM)
    blocks = [block for group in groups for block in group if block is not None]
    operands = [block_list, *blocks, *pieces] + ([] if begun is None else [begun])
    rows, width = blocks[0].shape[0], pieces[0].shape[1] // 2
    keep = jax.ShapeDtypeStruct((len(parts), rows, width), jnp.float32)
    full = jax.ShapeDtypeStruct((rows, 2 * width), jnp.float32)
    used = tuple(tuple(block is not None for block in group) for group in groups)
    return pl.pallas_call(
        functools.partial(
            multiply_kernel,
            groups=used,
            parts=parts,
            opening=opening,
            begun=begun is not None,
            width=width,
        ),
        out_shape=(keep, keep) + (full,) * len(opening),
        in_specs=[vmem] * len(operands),
        out_specs=(vmem,) * (2 + len(opening)),
        scratch_shapes=[pltpu.VMEM(full.shape, full.dtype)],
        cost_estimate=pl.CostEstimate(flops=cost, transcendentals=0, bytes_accessed=2**20),
        compiler_params=pltpu.CompilerParams(vmem_limit_bytes=8 * 2**20),
        name="multiply",
    )(*operands)


def add_kernel(*refs, terms):
    out, held, sems = refs[-3:]
    col = lax.axis_index("col")
    width = held.shape[2]
    copies = []
    for place, (part, kept, received) in enumerate(terms):
        held[place] = refs[kept[0]][kept[1]] + refs[received[0]][received[1]]
        start = pl.multiple_of((col ^ part) * width, width)
        copy = pltpu.make_async_copy(
            held.at[place], out.at[:, pl.ds(start, width)], sems.at[place]
        )
        copy.start()
        copies.append(copy)
    for copy in copies:
        copy.wait()


def add(sums, terms, earlier=None):
    anywhere = pl.BlockSpec(memory_space=pl.ANY)
    vmem = pl.BlockSpec(memory_space=pltpu.VMEM)
    rows, width = sums[0].shape[1:]
    aliased = [] if earlier is None else [earlier]
    return pl.pallas_call(
        functools.partial(add_kernel, terms=terms),
        out_shape=jax.ShapeDtypeStruct((rows, 4 * width), jnp.float32),
        in_specs=[vmem] * len(sums) + [anywhere] * len(aliased),
        out_specs=anywhere,
        scratch_shapes=[
            pltpu.VMEM((len(terms), rows, width), jnp.float32),
            pltpu.SemaphoreType.DMA((len(terms),)),
        ],
        input_output_aliases={len(sums): 0} if aliased else {},
        compiler_params=pltpu.CompilerParams(vmem_limit_bytes=8 * 2**20),
        name="add",
    )(*sums, *aliased)


def gather_shards(amps, ints, block_list):
    rows, cols = lax.axis_size("row"), lax.axis_size("col")
    col_pos = lax.axis_index("col")
    width = ints.shape[1] // cols

    def moved(block, target):
        route = [
            (r * cols + c, target(r, c)[0] * cols + target(r, c)[1])
            for r in range(rows)
            for c in range(cols)
        ]
        return lax.ppermute(block, GRID, route)

    def either(flip):
        return lambda r, c: (r ^ 1, c ^ 1) if (r >> 1 ^ c ^ flip) & 1 else (r ^ 2, c)

    first = functools.partial(moved, target=either(0))
    second = functools.partial(moved, target=either(1))
    across = functools.partial(moved, target=lambda r, c: (r, c ^ 2))
    beside = functools.partial(moved, target=lambda r, c: (r, c ^ 1))

    def chip_columns(chip):
        return lax.dynamic_slice_in_dim(ints, chip * 2 * width, 2 * width, 1)

    chip = col_pos // 2
    far0 = across(amps)
    near1 = first(amps)
    near2 = second(amps)
    pieces = [chip_columns(chip), across(chip_columns(1 - chip))]
    near3 = first(near1)
    far1 = first(far0)
    far0, near2 = lax.optimization_barrier((far0, near2))
    far2 = second(far0)
    far3 = first(far1)
    cost = 2 * 2 * amps.shape[0] * amps.shape[1] * width
    run = functools.partial(multiply, block_list, pieces=pieces)
    groups = [[amps, near1, near2, None], [far0, far1, far2, None]]
    keep, send = run(groups=groups, parts=(0, 2), cost=2 * cost)
    received = beside(send)
    groups = [[None, near1, near2, near3], [None, far1, far2, None]]
    keep1, send1, begun = run(groups=groups, parts=(1,), cost=cost, opening=(3,))
    received1 = beside(send1)
    groups = [[None, None, None, far3]]
    keep3, send3 = run(groups=groups, parts=(3,), cost=cost, begun=begun)
    received3 = beside(send3)
    sums = [keep, keep1, keep3, received, received1]
    out = add(sums, ((0, (0, 0), (4, 0)), (1, (1, 0), (3, 0)), (3, (2, 0), (3, 1))))
    out = add([keep, received3], ((2, (0, 1), (1, 0)),), out)
    return out[None]


def solution(mesh):
    placed = (P("col", "row"), P("col", "row"), P())
    whole_gather = mesh.shape["col"] == 4 and mesh.shape["row"] % 4 == 0
    return jax.shard_map(
        gather_shards if whole_gather else shift_shards,
        mesh=mesh,
        in_specs=placed,
        out_specs=P(("row", "col"), None, None),
        check_vma=False,
    )
```

```python
import functools

import jax
import jax.numpy as jnp
from jax import lax
from jax.experimental import pallas as pl
from jax.experimental.pallas import tpu as pltpu
from jax.sharding import PartitionSpec as P

GRID = ("row", "col")


def shifted(block, axis, distance):
    devices = range(lax.axis_size(axis))
    route = [((i - distance) % len(devices), i) for i in devices]
    return lax.ppermute(block, axis, route)


def shift_shards(amps, ints, block_list):
    row_pos = lax.axis_index("row")
    col_pos = lax.axis_index("col")
    col_count = lax.axis_size("col")
    running = jnp.zeros((amps.shape[0], ints.shape[1]), jnp.float32)
    held_amps = amps
    held_ints = ints
    for offset in range(col_count):
        block_id = (row_pos + col_pos - offset) % col_count
        factor = block_list[col_pos, block_id].astype(jnp.float32)
        running = running + factor * jnp.dot(
            held_amps, held_ints, preferred_element_type=jnp.float32
        )
        if offset + 1 < col_count:
            held_amps = shifted(held_amps, "row", 1)
            held_ints = shifted(held_ints, "col", 1)
    owned = lax.all_to_all(running, "col", split_axis=1, concat_axis=1, tiled=True)
    return owned.reshape(1, owned.shape[0], owned.shape[1])


def multiply_kernel(pairs, *refs, groups, parts, opening, begun, width):
    refs = list(refs)
    blocks = [[refs.pop(0) if used else None for used in group] for group in groups]
    pieces, refs = refs[:2], refs[2:]
    started = refs.pop(0) if begun else None
    keep, send, *opened, sums = refs
    row, col = lax.axis_index("row"), lax.axis_index("col")
    bit = lax.broadcasted_iota(jnp.int32, pairs.shape, 0) * 4
    bit = bit + lax.broadcasted_iota(jnp.int32, pairs.shape, 1)
    table = jnp.where(pairs[...] != 0, jnp.left_shift(1, bit), 0)
    table = jnp.sum(table.astype(jnp.float32)).astype(jnp.int32)
    mine = pl.multiple_of((col & 1) * width, width)
    other = pl.multiple_of(width - mine, width)
    turned = (((row >> 1) ^ col) & 1) == 1
    for index, part in enumerate(parts + opening):
        owner = col ^ part
        total = sums if index < len(parts) else opened[0]
        if begun and index == 0:
            total[...] = started[...]
        else:
            total[...] = jnp.zeros(total.shape, total.dtype)
        if part & 1 == 0:
            choices = ((0, 0, None), (1, 1, True), (1, 2, False))
        else:
            choices = ((0, 1, False), (0, 2, True), (1, 3, None))
        for slot, label, when_turned in choices:
            block = blocks[index][label]
            if block is None:
                continue
            kind = ((row ^ (2 * slot + (part & 1))) + owner) & 3
            listed = (lax.shift_right_logical(table, owner * 4 + kind) & 1) == 1
            if when_turned is not None:
                listed = listed & (turned if when_turned else ~turned)
            here = kind == ((row + col) & 3)
            for source in range(2):
                if part & 1 == 0 and source != (slot ^ (part >> 1)):
                    continue

                @pl.when(listed & (here == (source == 0)))
                def _(block=block, source=source, total=total):
                    total[...] += jnp.dot(
                        block[...], pieces[source][...], preferred_element_type=jnp.float32
                    )

        if index < len(parts):
            keep[index] = sums[:, pl.ds(mine, width)]
            send[index] = sums[:, pl.ds(other, width)]


def multiply(block_list, groups, pieces, parts, cost, opening=(), begun=None):
    vmem = pl.BlockSpec(memory_space=pltpu.VMEM)
    blocks = [block for group in groups for block in group if block is not None]
    operands = [block_list, *blocks, *pieces] + ([] if begun is None else [begun])
    rows, width = blocks[0].shape[0], pieces[0].shape[1] // 2
    keep = jax.ShapeDtypeStruct((len(parts), rows, width), jnp.float32)
    full = jax.ShapeDtypeStruct((rows, 2 * width), jnp.float32)
    used = tuple(tuple(block is not None for block in group) for group in groups)
    return pl.pallas_call(
        functools.partial(
            multiply_kernel,
            groups=used,
            parts=parts,
            opening=opening,
            begun=begun is not None,
            width=width,
        ),
        out_shape=(keep, keep) + (full,) * len(opening),
        in_specs=[vmem] * len(operands),
        out_specs=(vmem,) * (2 + len(opening)),
        scratch_shapes=[pltpu.VMEM(full.shape, full.dtype)],
        cost_estimate=pl.CostEstimate(flops=cost, transcendentals=0, bytes_accessed=2**20),
        compiler_params=pltpu.CompilerParams(vmem_limit_bytes=8 * 2**20),
        name="multiply",
    )(*operands)


def add_kernel(*refs, terms):
    out, held, sems = refs[-3:]
    col = lax.axis_index("col")
    width = held.shape[2]
    copies = []
    step = held.shape[1] // 2
    for place, (part, kept, received) in enumerate(terms):
        start = pl.multiple_of((col ^ part) * width, width)
        for piece in range(2):
            rows = pl.ds(piece * step, step)
            held[place, rows] = (
                refs[kept[0]][kept[1], rows] + refs[received[0]][received[1], rows]
            )
            copy = pltpu.make_async_copy(
                held.at[place, rows], out.at[rows, pl.ds(start, width)], sems.at[place, piece]
            )
            copy.start()
            copies.append(copy)
    for copy in copies:
        copy.wait()


def add(sums, terms, earlier=None):
    anywhere = pl.BlockSpec(memory_space=pl.ANY)
    vmem = pl.BlockSpec(memory_space=pltpu.VMEM)
    rows, width = sums[0].shape[1:]
    aliased = [] if earlier is None else [earlier]
    return pl.pallas_call(
        functools.partial(add_kernel, terms=terms),
        out_shape=jax.ShapeDtypeStruct((rows, 4 * width), jnp.float32),
        in_specs=[vmem] * len(sums) + [anywhere] * len(aliased),
        out_specs=anywhere,
        scratch_shapes=[
            pltpu.VMEM((len(terms), rows, width), jnp.float32),
            pltpu.SemaphoreType.DMA((len(terms), 2)),
        ],
        input_output_aliases={len(sums): 0} if aliased else {},
        compiler_params=pltpu.CompilerParams(vmem_limit_bytes=8 * 2**20),
        name="add",
    )(*sums, *aliased)


def gather_shards(amps, ints, block_list):
    rows, cols = lax.axis_size("row"), lax.axis_size("col")
    col_pos = lax.axis_index("col")
    width = ints.shape[1] // cols

    def moved(block, target):
        route = [
            (r * cols + c, target(r, c)[0] * cols + target(r, c)[1])
            for r in range(rows)
            for c in range(cols)
        ]
        return lax.ppermute(block, GRID, route)

    def either(flip):
        return lambda r, c: (r ^ 1, c ^ 1) if (r >> 1 ^ c ^ flip) & 1 else (r ^ 2, c)

    first = functools.partial(moved, target=either(0))
    second = functools.partial(moved, target=either(1))
    across = functools.partial(moved, target=lambda r, c: (r, c ^ 2))
    beside = functools.partial(moved, target=lambda r, c: (r, c ^ 1))

    def chip_columns(chip):
        return lax.dynamic_slice_in_dim(ints, chip * 2 * width, 2 * width, 1)

    chip = col_pos // 2
    far0 = across(amps)
    near1 = first(amps)
    near2 = second(amps)
    pieces = [chip_columns(chip), across(chip_columns(1 - chip))]
    near3 = first(near1)
    far1 = first(far0)
    far0, near2 = lax.optimization_barrier((far0, near2))
    far2 = second(far0)
    far3 = first(far1)
    cost = 2 * 2 * amps.shape[0] * amps.shape[1] * width
    run = functools.partial(multiply, block_list, pieces=pieces)
    groups = [[amps, near1, near2, None], [far0, far1, far2, None]]
    keep, send = run(groups=groups, parts=(0, 2), cost=2 * cost)
    received = beside(send)
    groups = [[None, near1, near2, near3], [None, far1, far2, None]]
    keep1, send1, begun = run(groups=groups, parts=(1,), cost=cost, opening=(3,))
    received1 = beside(send1)
    groups = [[None, None, None, far3]]
    keep3, send3 = run(groups=groups, parts=(3,), cost=cost, begun=begun)
    received3 = beside(send3)
    sums = [keep, keep1, keep3, received, received1]
    out = add(sums, ((0, (0, 0), (4, 0)), (1, (1, 0), (3, 0)), (3, (2, 0), (3, 1))))
    out = add([keep, received3], ((2, (0, 1), (1, 0)),), out)
    return out[None]


def solution(mesh):
    placed = (P("col", "row"), P("col", "row"), P())
    whole_gather = mesh.shape["col"] == 4 and mesh.shape["row"] % 4 == 0
    return jax.shard_map(
        gather_shards if whole_gather else shift_shards,
        mesh=mesh,
        in_specs=placed,
        out_specs=P(("row", "col"), None, None),
        check_vma=False,
    )
```
